32 devices in a mesh: chain: 4 (over x, core), band: 8 (over z, y).
Axes of the slice: x: 2, y: 2, z: 4, core: 2. Of those that a mesh axis runs over, the one named last changes fastest.
Arguments:
- diag_inverse: float32 [8192, 2048], P(('chain', 'band'))
- coupling: float32 [8192, 2048], P('chain', 'band'), may hold values from -0.09375 to 0.09375
- elem_stiff: float32 [24, 24, 16384], P(None, None, ('chain', 'band')), may hold values from -6 to 6
- elem_mass: float32 [24, 24, 16384], P(None, None, ('chain', 'band')), may hold values from -6 to 6
- elem_dofs: int32 [24, 16384], P(None, ('chain', 'band')), may hold values from 0 to 2047
- elem_slab: int32 [16384, 1], P(('chain', 'band')), may hold values from 0 to 3; in each aligned block of 512 rows (0 to 511, 512 to 1023, ...) at most 256 rows name the same one
- elem_var: int32 [16384], P(('chain', 'band')), may hold values from 0 to 191
- mode: float32 [8192], P(('chain', 'band')), may hold values from -0.4 to 0.4
- mass_mode: float32 [8192], P('chain'), may hold values from -1.2 to 1.2
- eigenvalue: float32 [1], replicated, may hold values from 0.5 to 2
Outputs:
- eigvec_slope: float32 [192, 8192], P(None, ('chain', 'band'))
- eigval_slope: float32 [192], replicated
The draws below stay inside these ranges and needn't reach their ends.
Inputs may be any that keep to these rules, and one draw needn't show every extreme that they name: `elem_slab`: within the rows of one device no slab is named by more than 256 elements, a bound that some block reaches.
All inputs are finite; a program needn't handle non-finite values.
Results may differ from the reference program's by a relative error of at most 0.00014.
Values sent between devices are 32-bit elements; how exact they have to be, the bound alone decides.
No kernel may reach another device: no remote copies, remote signals or barrier semaphores. Data moves between devices by JAX's collectives and lax.ppermute only.
A program may use at most 64 MiB of HBM per device.

```python
import math
import jax
import jax.numpy as jnp
import numpy as np
from jax import lax

B = 2048
ED = 24
VARS = 192
EL_DEV = 512
NDOF = 8192
ELEMS = 16384
CAP = 256
N_CHAIN = 4


def draw_diag_inverse(key, part):
    first_key, second_key = jax.random.split(jax.random.fold_in(key, 11))
    spread = jax.random.normal(first_key, (NDOF, B), jnp.float32) * (0.3 / B ** 0.5)
    diagonal = jax.random.uniform(second_key, (NDOF, 1), jnp.float32, minval=0.75, maxval=1.5)
    on_diagonal = jnp.arange(NDOF)[:, None] % B == jnp.arange(B)[None, :]
    return jnp.where(on_diagonal, diagonal, spread)


def with_ends(entries, stream_key, smallest, high):
    index_at = [jax.random.randint(jax.random.fold_in(stream_key, axis), (), 0, length) for axis, length in enumerate(entries.shape)]
    main_axis = entries.shape.index(max(entries.shape))
    beside = index_at[:main_axis] + [(index_at[main_axis] + 1) % entries.shape[main_axis]] + index_at[main_axis + 1:]
    return entries.at[tuple(index_at)].set(smallest).at[tuple(beside)].set(high)


def shard_levels(key, extent, cuts, smallest, high):
    def one(dim, blocks):
        draws = jax.random.uniform(jax.random.fold_in(jax.random.fold_in(key, 6), dim), (blocks,), jnp.float32, smallest / len(cuts), high / len(cuts))
        return jnp.repeat(jnp.exp(draws), extent[dim] // blocks).reshape((-1,) + (1,) * (len(extent) - dim - 1))

    level = one(*cuts[0])
    for cut in cuts[1:]:
        level = level * one(*cut)
    return level


def deal_out(key, own, number, rows, amount, top, bound, lean):
    order = jax.random.permutation(key, amount)
    packed, common = portions_of(amount, rows * top, bound, lean, True), portions_of(amount, rows * top, bound, lean, False)
    places = jnp.arange(amount)

    def named(lengths, offset_by):
        used = int((lengths > 0).sum())
        fixed = max(1, used // 4)
        shifted = fixed + (places - fixed + offset_by * (used - fixed)) % max(1, amount - fixed)
        return jnp.zeros((amount,), jnp.int32).at[order[jnp.where(places < fixed, places, shifted)]].set(jnp.asarray(lengths, jnp.int32))

    lengths = jnp.where(number % 4 == 0, named(packed, number // 4), named(common, number - number // 4 - 1))
    mixed = jax.random.permutation(jax.random.fold_in(own, 3), amount)
    giver, taker = mixed[0:amount // 2 * 2:2], mixed[1:amount // 2 * 2:2]
    room = jnp.minimum(lengths[giver] - 1, bound - lengths[taker]) // 2
    room = jnp.where((giver == order[0]) | (taker == order[0]) | (lengths[taker] == 0), 0, jnp.maximum(room, 0))
    shifted = jax.random.randint(jax.random.fold_in(own, 4), (amount // 2,), 0, 1 << 20) % (room + 1)
    lengths = lengths.at[giver].add(-shifted).at[taker].add(shifted)
    members = jnp.searchsorted(jnp.cumsum(lengths), jnp.arange(rows * top), side="right").astype(jnp.int32)
    listing = members.reshape(top, rows).T
    listing = listing[jax.random.permutation(jax.random.fold_in(own, 1), rows)]
    offset_by = jax.random.randint(jax.random.fold_in(own, 2), (rows, 1), 0, top)
    return jnp.take_along_axis(listing, (jnp.arange(top)[None, :] + offset_by) % top, axis=1)


def portions_of(number_of, total, reach, lean, full):
    weights = [(1 << 20) // math.isqrt(rank ** lean) + 1 for rank in range(1, number_of + 1)]
    largest = reach if full else min(reach, max(-(-total // number_of), total * weights[0] // sum(weights)))
    least = 1 if total - largest >= number_of - 1 else 0
    given, surplus = [largest] + [least] * (number_of - 1), total - largest - least * (number_of - 1)
    while surplus > 0:
        free = [i for i in range(1, number_of) if given[i] < largest] or [i for i in range(1, number_of) if given[i] < reach]
        whole, left = sum([weights[i] for i in free]), surplus
        for i in free:
            addition = min(reach - given[i], max(1, left * weights[i] // whole), surplus)
            given[i] = given[i] + addition
            surplus = surplus - addition
    return np.array(given)


def centred(key, extent, scale, most, shards=(), kind=jnp.bfloat16):
    loudness = shard_levels(key, extent, shards, -0.22, 0.18) if shards else 1.0
    values = jax.random.normal(key, extent, jnp.float32) * scale * loudness
    return jnp.minimum(jnp.maximum(values, -most), most).astype(kind)


def setup_inputs(seed: int = 0) -> dict:
    key_list = jax.random.split(jax.random.key(seed), 11)
    diag_inverse = draw_diag_inverse(jax.random.fold_in(key_list[10], 71), 0)
    coupling = centred(key_list[1], (NDOF, B), (2 * B) ** -0.5, 0.09375, ((0, 4), (1, 8)), jnp.float32)
    elem_stiff = centred(key_list[2], (ED, ED, ELEMS), 1.0, 6.0, ((2, 32),), jnp.float32)
    elem_mass = centred(key_list[3], (ED, ED, ELEMS), 1.0, 6.0, ((2, 32),), jnp.float32)
    elem_dofs = with_ends(jax.random.randint(key_list[4], (ED, ELEMS), 0, B), jax.random.fold_in(key_list[4], 1), 0, B - 1).astype(jnp.int32)
    elem_slab_keys = jax.random.split(jax.random.fold_in(key_list[5], 1), ELEMS // EL_DEV)
    elem_slab_turns = jax.random.permutation(jax.random.fold_in(key_list[5], 3), ELEMS // EL_DEV)
    elem_slab = jax.vmap(lambda own, number: deal_out(jax.random.fold_in(key_list[5], 2), own, number, EL_DEV, N_CHAIN, 1, CAP, 2))(elem_slab_keys, elem_slab_turns).reshape((ELEMS, 1))
    elem_var = with_ends(jax.random.randint(key_list[6], (ELEMS,), 0, VARS), jax.random.fold_in(key_list[6], 1), 0, VARS - 1).astype(jnp.int32)
    mode = centred(key_list[7], (NDOF,), 0.05, 0.4, ((0, 32),), jnp.float32)
    mass_mode = centred(key_list[8], (NDOF,), 0.15, 1.2, ((0, 4),), jnp.float32)
    eigenvalue = jnp.clip(jax.random.uniform(key_list[9], (1,), jnp.float32, 0.5, 2.0), 0.5, 2.0)
    return {"diag_inverse": diag_inverse, "coupling": coupling, "elem_stiff": elem_stiff, "elem_mass": elem_mass, "elem_dofs": elem_dofs, "elem_slab": elem_slab, "elem_var": elem_var, "mode": mode, "mass_mode": mass_mode, "eigenvalue": eigenvalue}


def reference(diag_inverse, coupling, elem_stiff, elem_mass, elem_dofs, elem_slab, elem_var, mode, mass_mode, eigenvalue):
    highest = lax.Precision.HIGHEST
    eigen_val = eigenvalue[0]
    dof_index = (elem_slab[:, 0][None, :] * B + elem_dofs).astype(jnp.int32)
    mode_at = mode[dof_index]
    operator = elem_stiff - eigen_val * elem_mass
    loads = -jnp.einsum("ije,je->ie", operator, mode_at, precision=highest)
    quadratic = -jnp.sum(mode_at * loads, axis=0)
    eigval_slope = jax.ops.segment_sum(quadratic, elem_var, num_segments=VARS)
    var_rows = jnp.broadcast_to(elem_var[None, :], dof_index.shape).astype(jnp.int32)
    rhs = jnp.zeros((VARS, NDOF), mode.dtype).at[var_rows, dof_index].add(loads)
    rhs = rhs + eigval_slope[:, None] * mass_mode[None, :]
    solved = []
    previous = jnp.zeros((VARS, B), mode.dtype)
    for slab_no in range(N_CHAIN):
        lower = slab_no * B
        coupled = rhs[:, lower:lower + B]
        if slab_no > 0:
            coupled = coupled - jnp.dot(previous, coupling[lower:lower + B].T, precision=highest)
        previous = jnp.dot(coupled, diag_inverse[lower:lower + B].T, precision=highest)
        solved.append(previous)
    results = [None] * N_CHAIN
    following = jnp.zeros((VARS, B), mode.dtype)
    for slab_no in range(N_CHAIN - 1, -1, -1):
        lower = slab_no * B
        remain = solved[slab_no]
        if slab_no < N_CHAIN - 1:
            upper = lower + B
            remain = remain - jnp.dot(following, coupling[upper:upper + B], precision=highest)
        following = jnp.dot(remain, diag_inverse[lower:lower + B], precision=highest)
        results[slab_no] = following
    eigvec_slope = jnp.concatenate(results, axis=1)
    return eigvec_slope, eigval_slope
```

```python
import functools

import jax
import jax.numpy as jnp
from jax import lax
from jax.experimental import pallas as pl
from jax.experimental.pallas import tpu as pltpu
from jax.sharding import PartitionSpec as P

VARS = 192
LANES = 128
CHUNK = 256
HBM = pl.BlockSpec(memory_space=pl.ANY)
VMEM = pl.BlockSpec(memory_space=pltpu.VMEM)
SMEM = pl.BlockSpec(memory_space=pltpu.SMEM)
NN = (((1,), (0,)), ((), ()))
NT = (((1,), (1,)), ((), ()))
BF16, F32, I32 = jnp.bfloat16, jnp.float32, jnp.int32


def round_up(n, m):
    return -(-n // m) * m


def halves(x):
    hi = x.astype(BF16)
    return hi, (x - hi.astype(F32)).astype(BF16)


def mul(a, b, dims):
    return lax.dot_general(a, b, dims, preferred_element_type=F32)


def mul3(a, b, dims):
    (ah, al), (bh, bl) = a, b
    return mul(ah, bh, dims) + (mul(al, bh, dims) + mul(ah, bl, dims))


def loads_kernel(groups, lam_ref, mode_ref, dofs_ref, slab_ref, var_ref, stiff_ref, mass_ref, out_ref, x_ref):
    width, count = dofs_ref.shape
    rows = mode_ref.shape[0]
    per_slab = rows // groups
    per_group = VARS // groups
    lam = lam_ref[0]
    dofs = dofs_ref[...]
    high = slab_ref[...] * per_slab + (dofs >> 7)
    low = dofs & (LANES - 1)
    spans = [slice(s, s + LANES) for s in range(0, count, LANES)]

    def look(r, found):
        row = jnp.broadcast_to(mode_ref[pl.ds(r, 1), :], (width, LANES))
        return tuple(
            jnp.where(high[:, s] == r, jnp.take_along_axis(row, low[:, s], axis=1), f)
            for s, f in zip(spans, found)
        )

    zero = jnp.zeros((width, LANES), F32)
    mode_at = jnp.concatenate(lax.fori_loop(0, rows, look, tuple(zero for _ in spans)), axis=1)
    quad = jnp.zeros((1, count), F32)
    x_ref[...] = jnp.zeros_like(x_ref)
    for i in range(width):
        load = -jnp.sum((stiff_ref[i] - lam * mass_ref[i]) * mode_at, axis=0, keepdims=True)
        quad = quad - mode_at[i : i + 1] * load
        x_ref[i : i + 1, :] = load
    var = var_ref[...]
    x_ref[width : 2 * width, :] = dofs.astype(F32)
    x_ref[2 * width : 2 * width + 1, :] = quad
    x_ref[2 * width + 1 : 2 * width + 2, :] = var.astype(F32)
    x_ref[2 * width + 2 : 2 * width + 3, :] = slab_ref[...].astype(F32)

    group = jnp.zeros_like(var)
    for g in range(1, groups):
        group = group + (var >= g * per_group).astype(I32)
    ids = lax.broadcasted_iota(I32, (8, count), 0)
    member = (ids == group).astype(F32)
    before = lax.broadcasted_iota(I32, (count, count), 0)
    after = lax.broadcasted_iota(I32, (count, count), 1)
    rank = mul(member.astype(BF16), (before < after).astype(F32).astype(BF16), NN)
    total = jnp.sum(member, axis=1, keepdims=True)
    offset = jnp.where(ids < group, total, 0.0)
    slot = jnp.sum(member * rank + offset, axis=0, keepdims=True).astype(I32)
    place = (before == slot).astype(F32).astype(BF16)
    x = x_ref[...]
    hi = x.astype(BF16)
    rest = x - hi.astype(F32)
    mid = rest.astype(BF16)
    low_part = (rest - mid.astype(F32)).astype(BF16)
    moved = mul(hi, place, NT) + (mul(mid, place, NT) + mul(low_part, place, NT))
    out_ref[...] = moved[: out_ref.shape[0]]


def element_loads(groups, lam, mode, dofs, slab, var, stiff, mass):
    width, count = dofs.shape
    features = round_up(2 * width + 3, 8)
    return pl.pallas_call(
        functools.partial(loads_kernel, groups),
        out_shape=jax.ShapeDtypeStruct((features, count), F32),
        in_specs=[SMEM] + [VMEM] * 6,
        out_specs=VMEM,
        scratch_shapes=[pltpu.VMEM((round_up(features, 16), count), F32)],
        name="loads",
    )(lam, mode, dofs, slab, var, stiff, mass)


def assemble_kernel(width, band, me_ref, feat_ref, mass_ref, first_ref, rest_ref, cols_ref, e_ref, v_ref, r_ref):
    sources, features, count = feat_ref.shape
    slabs, slab_cols = mass_ref.shape
    group_rows = VARS // sources
    piece = slab_cols // band
    me = me_ref[0]
    base = (me * group_rows).astype(F32)
    codes = v_ref.shape[1]
    nth = lax.broadcasted_iota(I32, (8, slab_cols), 1)
    code_at = lax.broadcasted_iota(I32, (8, codes), 1)
    e_ref_lanes = slab_cols + LANES

    def tile(s, t, filled):
        src = pl.ds(pl.multiple_of(t * 8, 8), 8)
        dst = pl.ds(pl.multiple_of(filled * 8, 8), 8)
        item = cols_ref[s, src, :]
        total = jnp.zeros((8, slab_cols), F32)
        for i in range(width):
            dof = item[:, width + i : width + i + 1].astype(I32)
            total = total + jnp.where(nth == dof, item[:, i : i + 1], 0.0)
        e_ref[dst, :slab_cols] = total
        e_ref[dst, slab_cols:] = jnp.broadcast_to(item[:, 2 * width : 2 * width + 1], (8, LANES))
        var = item[:, 2 * width + 1 : 2 * width + 2] - base
        slab = item[:, 2 * width + 2 : 2 * width + 3]
        held = (var >= 0.0) & (var < group_rows)
        code = jnp.where(held, slab * group_rows + var, -1.0).astype(I32)
        v_ref[dst, :] = (code_at == code).astype(F32)
        return filled + 1

    filled = jnp.int32(0)
    for s in range(sources):
        pad = cols_ref.shape[2] - features
        block = jnp.concatenate([feat_ref[s], jnp.zeros((pad, count), F32)], axis=0)
        cols_ref[s] = block.T
        var_row = feat_ref[s, 2 * width + 1 : 2 * width + 2, :]
        start = jnp.sum((var_row < base).astype(F32)).astype(I32)
        stop = jnp.sum((var_row < base + group_rows).astype(F32)).astype(I32)
        filled = lax.fori_loop(start >> 3, (stop + 7) >> 3, functools.partial(tile, s), filled)
    chunks = (filled * 8 + CHUNK - 1) // CHUNK

    def blank(t, _):
        dst = pl.ds(pl.multiple_of(t * 8, 8), 8)
        e_ref[dst, :] = jnp.zeros((8, e_ref_lanes), F32)
        v_ref[dst, :] = jnp.zeros((8, codes), F32)
        return 0

    lax.fori_loop(filled, chunks * (CHUNK // 8), blank, 0)
    r_ref[...] = jnp.zeros_like(r_ref)

    def gather(j, _):
        rows = pl.ds(pl.multiple_of(j * CHUNK, CHUNK), CHUNK)
        picks = v_ref[rows, :].T.astype(BF16)
        for lo in range(0, e_ref_lanes, 512):
            hi_ = min(lo + 512, e_ref_lanes)
            eh, el = halves(e_ref[rows, lo:hi_])
            r_ref[:, lo:hi_] += mul(picks, eh, NN) + mul(picks, el, NN)
        return 0

    lax.fori_loop(0, chunks, gather, 0)
    slope = jnp.zeros((group_rows, LANES), F32)
    for k in range(slabs):
        slope = slope + r_ref[k * group_rows : (k + 1) * group_rows, slab_cols:]
    for k in range(slabs):
        for b in range(band):
            span = slice(b * piece, (b + 1) * piece)
            part = r_ref[k * group_rows : (k + 1) * group_rows, span]
            part = part + slope[:, :1] * mass_ref[k : k + 1, span]
            if k == 0:
                first_ref[b, :group_rows, :] = part
            else:
                rest_ref[k - 1, b] = part
    r = lax.broadcasted_iota(I32, slope.shape, 0)
    l = lax.broadcasted_iota(I32, slope.shape, 1)
    slope_row = jnp.sum(jnp.where(r == l, slope, 0.0), axis=0, keepdims=True)
    tail = jnp.concatenate([slope_row] + [jnp.zeros((1, LANES), F32)] * (piece // LANES - 1), axis=1)
    for b in range(band):
        first_ref[b, group_rows:, :] = jnp.broadcast_to(tail, (8, piece))


def assemble(width, band, me, feats, mass):
    sources, features, count = feats.shape
    slabs, slab_cols = mass.shape
    group_rows = VARS // sources
    piece = slab_cols // band
    most = round_up(sources * (count + 8), CHUNK)
    codes = round_up(slabs * group_rows, LANES)
    return pl.pallas_call(
        functools.partial(assemble_kernel, width, band),
        out_shape=(
            jax.ShapeDtypeStruct((band, group_rows + 8, piece), F32),
            jax.ShapeDtypeStruct((slabs - 1, band, group_rows, piece), F32),
        ),
        in_specs=[SMEM, VMEM, VMEM],
        out_specs=(VMEM, VMEM),
        scratch_shapes=[
            pltpu.VMEM((sources, count, LANES), F32),
            pltpu.VMEM((most, slab_cols + LANES), F32),
            pltpu.VMEM((most, codes), F32),
            pltpu.VMEM((codes, slab_cols + LANES), F32),
        ],
        name="assemble",
    )(me, feats, mass)


def fetch(kinds, which, block, sem):
    for o, ref in enumerate(kinds):

        @pl.when(which == o)
        def _(ref=ref):
            pltpu.make_async_copy(ref, block, sem).start()


def landed(kinds, block, sem):
    pltpu.make_async_copy(kinds[0], block, sem).wait()


def forward_kernel(n, which_ref, full_ref, rhs_ref, *refs):
    diag, coup, (y_ref, send_ref, d_ref, c_ref, sems) = refs[:n], refs[n : 2 * n], refs[2 * n :]
    band, rows, piece = full_ref.shape
    fetch(diag, which_ref[0], d_ref, sems.at[0])
    fetch(coup, which_ref[1], c_ref, sems.at[1])
    landed(diag, d_ref, sems.at[0])
    y = jnp.zeros((rows, piece), F32)
    for b in range(band):
        span = slice(b * piece, (b + 1) * piece)
        y = y + mul3(halves(full_ref[b]), halves(d_ref[:, span]), NT)
    y_ref[...] = y
    yy = halves(y)
    landed(coup, c_ref, sems.at[1])
    for b in range(band):
        span = slice(b * piece, (b + 1) * piece)
        send_ref[b] = rhs_ref[b] - mul3(yy, halves(c_ref[span, :]), NT)


def turn_kernel(n, which_ref, full_ref, *refs):
    diag, (send_ref, d_ref, sems) = refs[:n], refs[n:]
    band, rows, piece = full_ref.shape
    fetch(diag, which_ref[0], d_ref, sems.at[0])
    landed(diag, d_ref, sems.at[0])
    y = jnp.zeros((rows, piece), F32)
    for b in range(band):
        span = slice(b * piece, (b + 1) * piece)
        y = y + mul3(halves(full_ref[b]), halves(d_ref[:, span]), NT)
    yy = halves(y)
    for b in range(band):
        span = slice(b * piece, (b + 1) * piece)
        send_ref[b] = mul3(yy, halves(d_ref[:, span]), NN)


def backward_kernel(n, which_ref, full_ref, y_ref, *refs):
    diag, coup, (send_ref, d_ref, c_ref, sems) = refs[:n], refs[n : 2 * n], refs[2 * n :]
    band, rows, piece = full_ref.shape
    fetch(coup, which_ref[1], c_ref, sems.at[1])
    fetch(diag, which_ref[0], d_ref, sems.at[0])
    landed(coup, c_ref, sems.at[1])
    left = y_ref[...]
    for b in range(band):
        span = slice(b * piece, (b + 1) * piece)
        left = left - mul3(halves(full_ref[b]), halves(c_ref[span, :]), NN)
    ll = halves(left)
    landed(diag, d_ref, sems.at[0])
    for b in range(band):
        span = slice(b * piece, (b + 1) * piece)
        send_ref[b] = mul3(ll, halves(d_ref[:, span]), NN)


def on_device(
    diag_inverse,
    coupling,
    elem_stiff,
    elem_mass,
    elem_dofs,
    elem_slab,
    elem_var,
    mode,
    mass_mode,
    eigenvalue,
):
    chain_len = lax.axis_size("chain")
    band_len = lax.axis_size("band")
    chain_pos = lax.axis_index("chain")
    band_pos = lax.axis_index("band")
    piece, slab_cols = diag_inverse.shape
    width, count = elem_dofs.shape
    group_rows = VARS // chain_len

    own_mass = lax.dynamic_slice_in_dim(mass_mode, band_pos * piece, piece, 0)
    both = jnp.stack([mode, own_mass])
    devices = chain_len * band_len
    tables = lax.all_to_all(
        jnp.broadcast_to(both[None], (devices,) + both.shape), ("chain", "band"), 0, 0, tiled=True
    )
    whole_mode = tables[:, 0].reshape(-1, LANES)
    whole_mass = tables[:, 1].reshape(chain_len, slab_cols)

    diag, coup = {0: diag_inverse}, {0: coupling}
    bit = chain_len // 2
    while bit:
        pairs = [(i, i ^ bit) for i in range(chain_len)]
        for held in (diag, coup):
            for o in list(held):
                held[o ^ bit] = lax.ppermute(held[o], "chain", pairs)
        bit //= 2
    diag = [diag[o] for o in range(chain_len)]
    coup = [coup[o] for o in range(chain_len)]

    feats = element_loads(
        chain_len,
        eigenvalue,
        whole_mode,
        elem_dofs,
        elem_slab.reshape(1, count),
        elem_var.reshape(1, count),
        elem_stiff,
        elem_mass,
    )
    gathered = lax.all_to_all(
        jnp.broadcast_to(feats[None], (chain_len,) + feats.shape), "chain", 0, 0, tiled=True
    )
    send, rest = assemble(width, band_len, chain_pos.reshape(1), gathered, whole_mass)

    def swap(blocks):
        return lax.all_to_all(blocks, "band", 0, 0, tiled=True)

    def spread(part):
        return swap(jnp.broadcast_to(part[None], (band_len,) + part.shape))

    panel = jax.ShapeDtypeStruct((band_len, group_rows, piece), F32)
    piece_of = jax.ShapeDtypeStruct((group_rows, piece), F32)
    d_scratch = pltpu.VMEM((piece, slab_cols), F32)
    c_scratch = pltpu.VMEM((slab_cols, piece), F32)
    sems = pltpu.SemaphoreType.DMA((2,))

    def which(d, c):
        return jnp.stack([chain_pos ^ d, chain_pos ^ c]).astype(I32)

    solved = []
    slope = None
    for k in range(chain_len):
        summed = jnp.sum(swap(send), axis=0)
        if k == 0:
            slope = summed[group_rows:]
            summed = summed[:group_rows]
        full = spread(summed)
        if k < chain_len - 1:
            y, send = pl.pallas_call(
                functools.partial(forward_kernel, chain_len),
                out_shape=(piece_of, panel),
                in_specs=[SMEM, VMEM, VMEM] + [HBM] * (2 * chain_len),
                out_specs=(VMEM, VMEM),
                scratch_shapes=[d_scratch, c_scratch, sems],
                name="forward",
            )(which(k, k + 1), full, rest[k], *diag, *coup)
            solved.append(y)
        else:
            send = pl.pallas_call(
                functools.partial(turn_kernel, chain_len),
                out_shape=panel,
                in_specs=[SMEM, VMEM] + [HBM] * chain_len,
                out_specs=VMEM,
                scratch_shapes=[d_scratch, sems],
                name="turn",
            )(which(k, k), full, *diag)
    results = [None] * chain_len
    for k in range(chain_len - 1, -1, -1):
        results[k] = jnp.sum(swap(send), axis=0)
        if k:
            send = pl.pallas_call(
                functools.partial(backward_kernel, chain_len),
                out_shape=panel,
                in_specs=[SMEM, VMEM, VMEM] + [HBM] * (2 * chain_len),
                out_specs=VMEM,
                scratch_shapes=[d_scratch, c_scratch, sems],
                name="backward",
            )(which(k - 1, k), spread(results[k]), solved[k - 1], *diag, *coup)

    outgoing = jnp.stack([jnp.concatenate([r, slope], axis=0) for r in results])
    arrived = lax.all_to_all(outgoing, "chain", 0, 0, tiled=True)
    eigvec_slope = arrived[:, :group_rows].reshape(VARS, piece)
    eigval_slope = arrived[:, group_rows, :group_rows].reshape(VARS)
    return (eigvec_slope, eigval_slope)


def solution(mesh):
    in_specs = (
        P(("chain", "band"), None),
        P("chain", "band"),
        P(None, None, ("chain", "band")),
        P(None, None, ("chain", "band")),
        P(None, ("chain", "band")),
        P(("chain", "band"), None),
        P(("chain", "band")),
        P(("chain", "band")),
        P("chain"),
        P(),
    )
    out_specs = (P(None, ("chain", "band")), P())
    return jax.shard_map(
        on_device, mesh=mesh, in_specs=in_specs, out_specs=out_specs, check_vma=False
    )
```
